32 devices in a mesh: groups: 2 (over y), tensor: 16 (over z, x, core).
Axes of the slice: x: 2, y: 2, z: 4, core: 2. Of those that a mesh axis runs over, the one named last changes fastest.
Arguments:
- normed_input: bfloat16 [16, 2, 8192], P('groups', None, 'tensor'), parts along dimension 0, may hold values from -6 to 6
- query_weight: bfloat16 [8192, 8192], P('tensor'), may hold values from -0.0625 to 0.0625
- query_gain: float32 [128], replicated, may hold values from 0.5 to 50
- image_cache: bfloat16 [32, 1601, 2048], P(('groups', 'tensor')), parts along dimension 0, may hold values from -18 to 18
- tile_count: int32 [16], P('groups'), parts along dimension 0, may hold values from 1 to 4, as said below
- image_first_slot: int32 [16], P('groups'), parts along dimension 0, may hold values from 0 to 15, as said below
- cross_tile_mask: int32 [16, 2, 4], P('groups'), parts along dimension 0, may hold values 0 or 1
- output_weight: bfloat16 [8192, 8192], P(None, 'tensor'), may hold values from -0.0625 to 0.0625
- output_gate: float32 [1], replicated, may hold values from 0.3 to 1.5
Outputs:
- cross_output: bfloat16 [16, 2, 8192], P('groups', None, 'tensor'), parts along dimension 0
The draws below stay inside these ranges and needn't reach their ends.
There are 2 independent parts, one for each index of `groups`. The reference program is written for one: setup_inputs(seed, part) draws one part's arguments, and reference() takes and returns one part's arrays. A program takes and returns all parts, laid end to end along the dimension named above; an argument that names none is the same for every part. Nothing has to cross between parts.
Inputs may be any that keep to these rules, and one draw needn't show every extreme that they name: tile_count sums to 16; some row has 4 tiles. Row r's tiles are pool slots image_first_slot[r] to image_first_slot[r] + tile_count[r] - 1; the images fill all 16 slots, each slot belonging to exactly one row.
All inputs are finite; a program needn't handle non-finite values.
Results may differ from the reference program's by a relative error of at most 0.0077.
Values may be sent and summed in bfloat16 or wider, within the bound.
A program may use at most 64 MiB of HBM per device.

```python
import math
import jax
import jax.numpy as jnp
from jax import lax

D = 8192
QH = 64
KVH = 8
HD = 128
TILE_TOK = 1601
MAX_TILES = 4
STEPS = 2
ROWS = 8
SLOTS = 16


def tile_layout(key):
    layout_key = jax.random.fold_in(key, 71)
    patterns = jnp.array([[4, 2, 1, 1], [1, 4, 1, 2], [2, 1, 1, 4], [1, 1, 4, 2], [2, 2, 2, 2], [3, 3, 1, 1], [1, 3, 2, 2], [3, 1, 1, 3]], dtype=jnp.int32)
    picked = jax.random.randint(jax.random.fold_in(layout_key, 1), (ROWS // 4,), 0, 8)
    picked = picked.at[0].set(picked[0] % 4)
    counts = jnp.take(patterns, picked, axis=0).reshape(ROWS)
    shuffle = jax.random.permutation(jax.random.fold_in(layout_key, 2), ROWS)
    counts = counts[shuffle]
    placing = jax.random.permutation(jax.random.fold_in(layout_key, 3), ROWS)
    ordered = counts[placing]
    single = jnp.argmax((ordered == 1).astype(jnp.int32)).astype(jnp.int32)
    last_row = placing[ROWS - 1]
    single_row = placing[single]
    placing = placing.at[single].set(last_row).at[ROWS - 1].set(single_row)
    ordered = counts[placing]
    starts_ordered = (jnp.cumsum(ordered) - ordered).astype(jnp.int32)
    starts = jnp.zeros((ROWS,), jnp.int32).at[placing].set(starts_ordered)
    return (counts.astype(jnp.int32), starts)


def draw_tile_count(key, part):
    return tile_layout(key)[0]


def draw_image_first_slot(key, part):
    return tile_layout(key)[1]


def draw_query_gain(key, part):
    gains = jnp.exp(jax.random.uniform(key, (HD,), minval=math.log(0.5), maxval=math.log(3.0)))
    return gains.astype(jnp.float32)


def draw_image_cache(key, part):
    key_keys, key_scale, key_values = jax.random.split(key, 3)
    width = KVH * HD
    token_scale = jnp.exp(jax.random.uniform(key_scale, (SLOTS, TILE_TOK, 1), minval=math.log(0.3), maxval=math.log(3.0)))
    keys = jnp.clip(jax.random.normal(key_keys, (SLOTS, TILE_TOK, width)), -6.0, 6.0) * token_scale
    values = 2.0 * jnp.clip(jax.random.normal(key_values, (SLOTS, TILE_TOK, width)), -6.0, 6.0)
    return jnp.concatenate([keys, values], axis=-1).astype(jnp.bfloat16)


def touch_ends(values, key, least, largest):
    longest = values.shape.index(max(values.shape))
    spots = []
    for shift in (0, 1):
        where = [jax.random.randint(jax.random.fold_in(key, axis), (), 0, length) for axis, length in enumerate(values.shape)]
        where[longest] = (where[longest] + shift) % values.shape[longest]
        spots.append(tuple(where))
    return values.at[spots[0]].set(least).at[spots[1]].set(largest)


def block_levels(stream_key, shape, cuts, least, largest):
    def one(axis_at, blocks):
        draws = jax.random.uniform(jax.random.fold_in(jax.random.fold_in(stream_key, 6), axis_at), (blocks,), jnp.float32, least / len(cuts), largest / len(cuts))
        return jnp.repeat(jnp.exp(draws), shape[axis_at] // blocks).reshape((-1,) + (1,) * (len(shape) - axis_at - 1))

    loudness = one(*cuts[0])
    for cut in cuts[1:]:
        loudness = loudness * one(*cut)
    return loudness


def scatter_about(stream_key, extent, deviation, bound, shards=(), kind=jnp.bfloat16):
    values = deviation * jax.random.normal(stream_key, extent, jnp.float32)
    if shards:
        values = values * block_levels(stream_key, extent, shards, -0.22, 0.18)
    return jnp.clip(values, -bound, bound).astype(kind)


def setup_inputs(seed: int = 0, part: int = 0) -> dict:
    arg_keys = jax.random.split(jax.random.key(seed), 10)
    part_keys = jax.random.split(jax.random.fold_in(arg_keys[9], part), 10)
    return {
        "normed_input": scatter_about(part_keys[0], (ROWS, STEPS, D), 1.0, 6.0, ((2, 16),)),
        "query_weight": scatter_about(arg_keys[1], (D, QH * HD), D ** -0.5, 0.0625, ((0, 16),)),
        "query_gain": draw_query_gain(jax.random.fold_in(arg_keys[9], 71), part),
        "image_cache": draw_image_cache(jax.random.fold_in(jax.random.fold_in(arg_keys[9], part), 71), part),
        "tile_count": draw_tile_count(jax.random.fold_in(jax.random.fold_in(arg_keys[9], part), 71), part),
        "image_first_slot": draw_image_first_slot(jax.random.fold_in(jax.random.fold_in(arg_keys[9], part), 71), part),
        "cross_tile_mask": touch_ends((jax.random.randint(part_keys[6], (ROWS, STEPS, MAX_TILES), 0, 2) < 1).astype(jnp.int32), jax.random.fold_in(part_keys[6], 1), 0, 1),
        "output_weight": scatter_about(arg_keys[7], (QH * HD, D), (QH * HD) ** -0.5, 0.0625, ((1, 16),)),
        "output_gate": jnp.clip(jax.random.uniform(arg_keys[8], (1,), jnp.float32, 0.3, 1.5), 0.3, 1.5),
    }


EPSILON = 1e-05
NEGATIVE_FLOOR = -1e+30

def membership(image_first_slot, tile_count, pool_slots):
    ends = image_first_slot + tile_count
    return (pool_slots[:, None] >= image_first_slot[None, :]) & (pool_slots[:, None] < ends[None, :])

def active_status(member_flag, image_first_slot, cross_tile_mask, pool_slots):
    member_int = member_flag.astype(jnp.int32)
    tile_index = lax.optimization_barrier(jnp.sum(member_int * (pool_slots[:, None] - image_first_slot[None, :]), axis=1))
    row_masks = lax.optimization_barrier(jnp.sum(member_int[:, :, None, None] * cross_tile_mask[None], axis=1))
    positions = jnp.arange(cross_tile_mask.shape[2], dtype=jnp.int32)
    chosen = lax.optimization_barrier(jnp.sum(jnp.where(positions[None, None, :] == tile_index[:, None, None], row_masks, 0), axis=2))
    return (tile_index[:, None] == 0) | (chosen == 1)

def tile_partial(query_rows, cache_tile):
    steps = query_rows.shape[0]
    kv_width = cache_tile.shape[1] // 2
    kv_heads = kv_width // HD
    group = query_rows.shape[1] // kv_width
    grouped = query_rows.reshape(steps, kv_heads, group, HD).astype(jnp.float32)
    keys = cache_tile[:, :kv_width].reshape(-1, kv_heads, HD).astype(jnp.float32)
    values = cache_tile[:, kv_width:].reshape(-1, kv_heads, HD).astype(jnp.float32)
    scores = jnp.einsum('skgd,tkd->skgt', grouped, keys) * (1.0 / math.sqrt(HD))
    tops = lax.optimization_barrier(jnp.max(scores, axis=3))
    weights = jnp.exp(scores - tops[..., None]).astype(jnp.bfloat16).astype(jnp.float32)
    totals = lax.optimization_barrier(jnp.sum(weights, axis=3))
    mixed = jnp.einsum('skgt,tkd->skgd', weights, values)
    return (tops.reshape(steps, -1), totals.reshape(steps, -1), mixed.reshape(steps, -1))

def slot_term(operands):
    return tile_partial(operands[0], operands[1])

def reference(normed_input, query_weight, query_gain, image_cache, tile_count, image_first_slot, cross_tile_mask, output_weight, output_gate):
    flattened = normed_input.reshape(ROWS * STEPS, D)
    query = jnp.dot(flattened, query_weight, preferred_element_type=jnp.float32)
    heads = query.reshape(ROWS * STEPS, QH, HD)
    normed = heads * lax.rsqrt(lax.optimization_barrier(jnp.mean(heads * heads, axis=2, keepdims=True)) + EPSILON) * query_gain
    normed = normed.astype(jnp.bfloat16).reshape(ROWS, STEPS * QH * HD)
    pool_slots = jnp.arange(SLOTS, dtype=jnp.int32)
    member_flag = membership(image_first_slot, tile_count, pool_slots)
    active_entry = active_status(member_flag, image_first_slot, cross_tile_mask, pool_slots)
    selected = jnp.dot(member_flag.astype(jnp.bfloat16), normed, preferred_element_type=jnp.float32)
    selected = selected.astype(jnp.bfloat16).reshape(SLOTS, STEPS, QH * HD)
    tops, totals, mixed = lax.map(slot_term, (selected, image_cache))
    masked = jnp.where(active_entry[:, :, None], tops, NEGATIVE_FLOOR)
    row_max = lax.optimization_barrier(jnp.max(jnp.where(member_flag[:, :, None, None], masked[:, None], NEGATIVE_FLOOR), axis=0))
    slot_max = lax.optimization_barrier(jnp.max(jnp.where(member_flag[:, :, None, None], row_max[None], NEGATIVE_FLOOR), axis=1))
    factor = jnp.where(active_entry[:, :, None], jnp.exp(masked - slot_max), 0.0)
    numer = (mixed.reshape(SLOTS, STEPS, QH, HD) * factor[..., None]).reshape(SLOTS, STEPS * QH * HD)
    denom = (totals * factor).reshape(SLOTS, STEPS * QH)
    member_float = member_flag.astype(jnp.float32).T
    numer_rows = jnp.dot(member_float, numer, precision=lax.Precision.HIGHEST).reshape(ROWS * STEPS, QH, HD)
    denom_rows = jnp.dot(member_float, denom, precision=lax.Precision.HIGHEST).reshape(ROWS * STEPS, QH)
    attended = (numer_rows / denom_rows[..., None]).astype(jnp.bfloat16).reshape(ROWS * STEPS, QH * HD)
    projected = jnp.dot(attended, output_weight, preferred_element_type=jnp.float32)
    result = jnp.tanh(output_gate[0]) * projected
    return result.astype(jnp.bfloat16).reshape(ROWS, STEPS, D)
```

```python
import functools
import math

import jax
import jax.numpy as jnp
from jax import lax
from jax.experimental import pallas as pl
from jax.experimental.pallas import tpu as pltpu
from jax.sharding import PartitionSpec as P

EPSILON = 1e-05
NEGATIVE_FLOOR = -1e30
MESH = pl.DeviceIdType.MESH


def membership(image_first_slot, tile_count, pool_slots):
    ends = image_first_slot + tile_count
    return (pool_slots[:, None] >= image_first_slot[None, :]) & (
        pool_slots[:, None] < ends[None, :]
    )


def active_status(member_flag, image_first_slot, cross_tile_mask, pool_slots):
    member_int = member_flag.astype(jnp.int32)
    tile_index = jnp.sum(member_int * (pool_slots[:, None] - image_first_slot[None, :]), axis=1)
    row_masks = jnp.sum(member_int[:, :, None, None] * cross_tile_mask[None], axis=1)
    positions = jnp.arange(cross_tile_mask.shape[2], dtype=jnp.int32)
    chosen = jnp.sum(
        jnp.where(positions[None, None, :] == tile_index[:, None, None], row_masks, 0), axis=2
    )
    return (tile_index[:, None] == 0) | (chosen == 1)


def tile_partial(query_rows, cache_tile, head_size):
    steps = query_rows.shape[0]
    kv_width = cache_tile.shape[1] // 2
    kv_heads = kv_width // head_size
    group = query_rows.shape[1] // kv_width
    grouped = query_rows.reshape(steps, kv_heads, group, head_size)
    keys = cache_tile[:, :kv_width].reshape(-1, kv_heads, head_size)
    values = cache_tile[:, kv_width:].reshape(-1, kv_heads, head_size)
    scores = jnp.einsum("skgd,tkd->skgt", grouped, keys, preferred_element_type=jnp.float32) * (
        1.0 / math.sqrt(head_size)
    )
    tops = jnp.max(scores, axis=3)
    weights = jnp.exp(scores - tops[..., None]).astype(jnp.bfloat16)
    totals = jnp.sum(weights.astype(jnp.float32), axis=3)
    mixed = jnp.einsum("skgt,tkd->skgd", weights, values, preferred_element_type=jnp.float32)
    return (tops.reshape(steps, -1), totals.reshape(steps, -1), mixed.reshape(steps, -1))


def finish(numer_pairs, denom_pairs, head_size):
    pairs = numer_pairs.shape[0]
    heads = denom_pairs.shape[1]
    shaped = numer_pairs.reshape(pairs, heads, head_size) / denom_pairs[..., None]
    return shaped.astype(jnp.bfloat16).reshape(pairs, heads * head_size)


def body(
    normed_input,
    query_weight,
    query_gain,
    image_cache,
    tile_count,
    image_first_slot,
    cross_tile_mask,
    output_weight,
    output_gate,
):
    rows, steps, local_width = normed_input.shape
    head_size = query_gain.shape[0]
    heads = query_weight.shape[1] // head_size
    slot_count = image_cache.shape[0]
    flattened = normed_input.reshape(rows * steps, local_width)
    query = lax.psum_scatter(
        jnp.dot(flattened, query_weight, preferred_element_type=jnp.float32),
        "tensor",
        scatter_dimension=0,
        tiled=True,
    )
    shaped = query.reshape(slot_count, heads, head_size)
    normed = (
        shaped * lax.rsqrt(jnp.mean(shaped * shaped, axis=2, keepdims=True) + EPSILON) * query_gain
    )
    normed = normed.astype(jnp.bfloat16).reshape(slot_count, heads * head_size)
    all_queries = lax.all_gather(normed, "tensor", axis=0, tiled=True)
    target_device = lax.axis_index("tensor")
    pool_slots = target_device * slot_count + jnp.arange(slot_count, dtype=jnp.int32)
    member_flag = membership(image_first_slot, tile_count, pool_slots)
    active_entry = active_status(member_flag, image_first_slot, cross_tile_mask, pool_slots)
    by_row = all_queries.reshape(rows, steps * heads * head_size)
    selected = jnp.dot(member_flag.astype(jnp.bfloat16), by_row, preferred_element_type=jnp.float32)
    selected = selected.astype(jnp.bfloat16).reshape(slot_count, steps, heads * head_size)

    def slot_term(operands):
        return tile_partial(operands[0], operands[1], head_size)

    tops, totals, mixed = lax.map(slot_term, (selected, image_cache))
    masked = jnp.where(active_entry[:, :, None], tops, NEGATIVE_FLOOR)
    pair_index = target_device * slot_count + jnp.arange(slot_count, dtype=jnp.int32)
    pair_row = pair_index // steps
    pair_step = pair_index % steps
    gathered_tops, gathered_totals, gathered_mixed = (
        lax.all_gather(masked, "tensor", axis=0, tiled=True),
        lax.all_gather(totals, "tensor", axis=0, tiled=True),
        lax.all_gather(mixed, "tensor", axis=0, tiled=True),
    )
    all_slots = gathered_tops.shape[0]
    every_slot = jnp.arange(all_slots, dtype=jnp.int32)
    full_member = membership(image_first_slot, tile_count, every_slot)
    slot_pick = full_member[:, pair_row]
    step_pick = jnp.arange(steps, dtype=jnp.int32)[None, :] == pair_step[:, None]
    chosen = slot_pick[:, :, None] & step_pick[None, :, :]
    spread = jnp.where(chosen[..., None], gathered_tops[:, None, :, :], NEGATIVE_FLOOR)
    pair_max = jnp.max(spread, axis=(0, 2))
    weights = jnp.where(chosen[..., None], jnp.exp(spread - pair_max[None, :, None, :]), 0.0)
    denom_pairs = jnp.sum(weights * gathered_totals[:, None, :, :], axis=(0, 2))
    mixed_heads = gathered_mixed.reshape(all_slots, steps, heads, head_size)
    numer_pairs = jnp.einsum(
        "spth,sthd->phd", weights, mixed_heads, precision=lax.Precision.HIGHEST
    )
    numer_pairs = numer_pairs.reshape(slot_count, heads * head_size)
    attended = finish(numer_pairs, denom_pairs, head_size)
    projected = jnp.dot(
        lax.all_gather(attended, "tensor", axis=0, tiled=True),
        output_weight,
        preferred_element_type=jnp.float32,
    )
    result = jnp.tanh(output_gate[0]) * projected
    return result.astype(jnp.bfloat16).reshape(rows, steps, -1)


def fused_kernel(
    count_ref, first_ref, mask_ref, x_ref, gain_ref, wq_hbm, cache_hbm, wo_hbm, out_ref,
    wq_s, kv_s, wo_s, send_a, recv_a, send_b, recv_b, send_c, recv_c, send_e, recv_e, live_s, att_s, att_all,
    wq_sem, kv_sem, wo_sem, a_send, a_recv, b_send, b_recv, c_send, c_recv, e_send, e_recv,
    f_send, f_recv, p_send, p_recv,
    *, devices, kv_heads, steps, head_size,
):
    chips = devices // 2
    me = lax.axis_index("tensor")
    core = lax.rem(me, 2)
    chip = lax.div(me, 2)
    partner = me + 1 - 2 * core
    pairs, _ = x_ref.shape
    rows = pairs // steps
    width = wq_s.shape[2]
    local_heads = width // head_size
    tile = local_heads * steps
    block = rows * tile

    def remote(src, dst, send_sem, recv_sem, device):
        return pltpu.make_async_remote_copy(
            src_ref=src, dst_ref=dst, send_sem=send_sem, recv_sem=recv_sem,
            device_id={"tensor": device}, device_id_type=MESH,
        )

    def at(index, size):
        return pl.ds(pl.multiple_of(index * size, size), size)

    ahead = [lax.rem(chip + 1 + i, chips) for i in range(chips)]
    behind = [lax.rem(chip + 2 * chips - 1 - i, chips) for i in range(chips)]
    order = [2 * c + 1 - core for c in ahead] + [2 * c + core for c in ahead]
    wq_copies = [
        pltpu.make_async_copy(wq_hbm.at[:, at(b, width)], wq_s.at[n], wq_sem.at[n])
        for n, b in enumerate(order)
    ]
    for copy in wq_copies:
        copy.start()

    barrier = pltpu.get_barrier_semaphore()
    for j in range(1, devices):
        pl.semaphore_signal(
            barrier, inc=1, device_id={"tensor": lax.rem(me + j, devices)}, device_id_type=MESH
        )
    pl.semaphore_wait(barrier, devices - 1)

    x = x_ref[...]
    a_copies = [
        remote(send_a.at[i], recv_a.at[i], a_send.at[i], a_recv.at[i], partner) for i in range(chips)
    ]
    b_copies = [
        remote(send_b.at[i], recv_b.at[i], b_send.at[i], b_recv.at[i], 2 * ahead[i] + core)
        for i in range(chips - 1)
    ]
    for i in range(chips):
        wq_copies[i].wait()
        send_a[i] = jnp.dot(x, wq_s[i], preferred_element_type=jnp.float32)
        a_copies[i].start()
    query = None
    for i in range(chips):
        wq_copies[chips + i].wait()
        mine = jnp.dot(x, wq_s[chips + i], preferred_element_type=jnp.float32)
        a_copies[i].wait_recv()
        total = mine + recv_a[i]
        if i < chips - 1:
            send_b[i] = total
            b_copies[i].start()
        else:
            query = total

    kv_copy = pltpu.make_async_copy(cache_hbm.at[0], kv_s, kv_sem.at[0])
    kv_copy.start()
    wo_copy = pltpu.make_async_copy(wo_hbm, wo_s, wo_sem.at[0])
    wo_copy.start()

    shape = (devices * tile, pairs)
    row_at = lax.broadcasted_iota(jnp.int32, shape, 0)
    pair_at = lax.broadcasted_iota(jnp.int32, shape, 1)
    slot_at = row_at >> (tile.bit_length() - 1)
    inner = row_at & (tile - 1)
    step_at = inner & (steps - 1)
    head_at = inner >> (steps.bit_length() - 1)
    row_of = jnp.zeros(shape, jnp.int32)
    for r in range(rows):
        low = first_ref[r]
        row_of = jnp.where((slot_at >= low) & (slot_at < low + count_ref[r]), r, row_of)
    wanted = row_of * steps + step_at == pair_at

    whole = (devices, tile, head_size)
    slot_at = lax.broadcasted_iota(jnp.int32, whole, 0)
    step_at = lax.broadcasted_iota(jnp.int32, whole, 1) & (steps - 1)
    live_row = jnp.full(whole, -1, jnp.int32)
    for r in range(rows):
        tile_at = slot_at - first_ref[r]
        allowed = jnp.where(tile_at == 0, 1, 0)
        for t in range(1, mask_ref.shape[1]):
            for s in range(steps):
                allowed = jnp.where((tile_at == t) & (step_at == s), mask_ref[s, t, r], allowed)
        live_row = jnp.where((tile_at < count_ref[r]) & (allowed == 1), r, live_row)
    live_s[...] = live_row

    for i in range(chips - 1):
        b_copies[i].wait_recv()
        query = query + recv_b[i]
    gain = gain_ref[...]
    routed = jnp.zeros((devices * tile, head_size), jnp.float32)
    for h in range(local_heads):
        part = query[:, h * head_size : (h + 1) * head_size]
        mean = jnp.mean(part * part, axis=1, keepdims=True)
        normed = (part * lax.rsqrt(mean + EPSILON) * gain).astype(jnp.bfloat16)
        pick = jnp.where(wanted & (head_at == h), 1.0, 0.0).astype(jnp.bfloat16)
        routed = routed + jnp.dot(pick, normed, preferred_element_type=jnp.float32)
    send_c[...] = routed
    c_copies = []
    for j in range(1, devices):
        device = lax.rem(me + j, devices)
        c_copies.append(
            remote(
                send_c.at[at(device, tile)], recv_c.at[at(me, tile)],
                c_send.at[j], c_recv.at[j], device,
            )
        )
        c_copies[-1].start()
    recv_c[at(me, tile), :] = send_c[at(me, tile), :]
    kv_copy.wait()
    for copy in c_copies:
        copy.wait_recv()

    q_all = recv_c[...].astype(jnp.bfloat16)
    group_rows = devices * tile // kv_heads
    kv_width = kv_heads * head_size
    lane = lax.broadcasted_iota(jnp.int32, (group_rows, head_size), 1)
    for g in range(kv_heads):
        keys = kv_s[:, g * head_size : (g + 1) * head_size]
        values = kv_s[:, kv_width + g * head_size : kv_width + (g + 1) * head_size]
        scores = lax.dot_general(
            q_all[g * group_rows : (g + 1) * group_rows], keys, (((1,), (1,)), ((), ())),
            preferred_element_type=jnp.float32,
        ) * (1.0 / math.sqrt(head_size))
        top = jnp.max(scores, axis=1, keepdims=True)
        weights = jnp.exp(scores - top).astype(jnp.bfloat16)
        sums = jnp.sum(weights.astype(jnp.float32), axis=1, keepdims=True)
        mixed = jnp.dot(weights, values, preferred_element_type=jnp.float32)
        stats = jnp.where(lane < head_size // 2, top, sums)
        for n in range(group_rows // tile):
            d = g * (group_rows // tile) + n
            send_e[d, :tile, :] = mixed[n * tile : (n + 1) * tile]
            send_e[d, tile:, :] = stats[n * tile : (n + 1) * tile]
    e_copies = []
    for j in range(1, devices):
        device = lax.rem(me + j, devices)
        e_copies.append(
            remote(
                send_e.at[device], recv_e.at[me], e_send.at[j], e_recv.at[j], device,
            )
        )
        e_copies[-1].start()
    recv_e[me] = send_e[me]
    for copy in e_copies:
        copy.wait_recv()

    mixes = recv_e[:, :tile, :]
    stats = recv_e[:, tile:, :]
    whole = (devices, tile, head_size)
    tops = jnp.broadcast_to(stats[:, :, 0:1], whole)
    sums = jnp.broadcast_to(stats[:, :, head_size // 2 : head_size // 2 + 1], whole)
    live_row = live_s[...]
    peaks = jnp.zeros(whole, jnp.float32)
    for r in range(rows):
        here = live_row == r
        peak = jnp.max(jnp.where(here, tops, NEGATIVE_FLOOR), axis=0, keepdims=True)
        peaks = jnp.where(here, peak, peaks)
    alive = live_row >= 0
    factor = jnp.where(alive, jnp.exp(jnp.where(alive, tops - peaks, 0.0)), 0.0)
    mixes = factor * mixes
    sums = factor * sums
    for r in range(rows):
        here = live_row == r
        numer = jnp.sum(jnp.where(here, mixes, 0.0), axis=0)
        denom = jnp.sum(jnp.where(here, sums, 0.0), axis=0)
        att_s[r * tile : (r + 1) * tile, :] = numer / denom

    to = lax.broadcasted_iota(jnp.int32, (block, block), 0)
    fro = lax.broadcasted_iota(jnp.int32, (block, block), 1)
    to_head = to >> (pairs.bit_length() - 1)
    to_pair = to & (pairs - 1)
    source = (
        (to_pair >> (steps.bit_length() - 1)) * tile + to_head * steps + (to_pair & (steps - 1))
    )
    swap = jnp.where(source == fro, 1.0, 0.0).astype(jnp.bfloat16)
    att_all[at(me, block), :] = jnp.dot(
        swap, att_s[...].astype(jnp.bfloat16), preferred_element_type=jnp.float32
    ).astype(jnp.bfloat16)

    f_copies = [
        remote(
            att_all.at[at(me, block)], att_all.at[at(me, block)],
            f_send.at[i], f_recv.at[i], 2 * ahead[i] + core,
        )
        for i in range(chips - 1)
    ]
    arrived = [me] + [2 * behind[i] + core for i in range(chips - 1)]
    p_copies = [
        remote(
            att_all.at[at(b, block)], att_all.at[at(b, block)], p_send.at[n], p_recv.at[n], partner
        )
        for n, b in enumerate(arrived)
    ]
    p_copies[0].start()
    for copy in f_copies:
        copy.start()
    wo_copy.wait()

    def projected(b):
        heads = att_all[at(b, block), :]
        joined = jnp.concatenate(
            [heads[h * pairs : (h + 1) * pairs] for h in range(local_heads)], axis=1
        )
        return jnp.dot(joined, wo_s[at(b, width), :], preferred_element_type=jnp.float32)

    result = projected(me)
    for i in range(chips - 1):
        f_copies[i].wait_recv()
        p_copies[i + 1].start()
        result = result + projected(arrived[i + 1])
    for n in range(chips):
        p_copies[n].wait_recv()
        result = result + projected(arrived[n] + 1 - 2 * core)
    out_ref[...] = result
    for copy in a_copies + b_copies + c_copies + e_copies + f_copies + p_copies:
        copy.wait_send()


def fused_body(
    devices,
    normed_input,
    query_weight,
    query_gain,
    image_cache,
    tile_count,
    image_first_slot,
    cross_tile_mask,
    output_weight,
    output_gate,
):
    rows, steps, local_width = normed_input.shape
    head_size = query_gain.shape[0]
    tokens, cache_width = image_cache.shape[1:]
    width = query_weight.shape[1] // devices
    pairs = rows * steps
    tile = width // head_size * steps
    chips = devices // 2
    dma = pltpu.SemaphoreType.DMA
    smem = pl.BlockSpec(memory_space=pltpu.SMEM)
    vmem = pl.BlockSpec(memory_space=pltpu.VMEM)
    hbm = pl.BlockSpec(memory_space=pl.ANY)
    result = pl.pallas_call(
        functools.partial(
            fused_kernel, devices=devices, kv_heads=cache_width // 2 // head_size, steps=steps,
            head_size=head_size,
        ),
        out_shape=jax.ShapeDtypeStruct((pairs, output_weight.shape[1]), jnp.float32),
        in_specs=[smem, smem, smem, vmem, vmem, hbm, hbm, hbm],
        out_specs=vmem,
        scratch_shapes=[
            pltpu.VMEM((devices, local_width, width), jnp.bfloat16),
            pltpu.VMEM((tokens, cache_width), jnp.bfloat16),
            pltpu.VMEM(output_weight.shape, jnp.bfloat16),
            pltpu.VMEM((chips, pairs, width), jnp.float32),
            pltpu.VMEM((chips, pairs, width), jnp.float32),
            pltpu.VMEM((chips - 1, pairs, width), jnp.float32),
            pltpu.VMEM((chips - 1, pairs, width), jnp.float32),
            pltpu.VMEM((devices * tile, head_size), jnp.float32),
            pltpu.VMEM((devices * tile, head_size), jnp.float32),
            pltpu.VMEM((devices, 2 * tile, head_size), jnp.float32),
            pltpu.VMEM((devices, 2 * tile, head_size), jnp.float32),
            pltpu.VMEM((devices, tile, head_size), jnp.int32),
            pltpu.VMEM((rows * tile, head_size), jnp.float32),
            pltpu.VMEM((devices * rows * tile, head_size), jnp.bfloat16),
            dma((devices,)), dma((1,)), dma((1,)),
            dma((chips,)), dma((chips,)), dma((chips,)), dma((chips,)),
            dma((devices,)), dma((devices,)), dma((devices,)), dma((devices,)),
            dma((chips,)), dma((chips,)), dma((chips,)), dma((chips,)),
        ],
        compiler_params=pltpu.CompilerParams(collective_id=0, has_side_effects=True),
        name="gated_cross_attention",
    )(
        tile_count, image_first_slot, cross_tile_mask.transpose(1, 2, 0), normed_input.reshape(pairs, local_width),
        query_gain.reshape(1, head_size), query_weight, image_cache, output_weight,
    )
    result = jnp.tanh(output_gate[0]) * result
    return result.astype(jnp.bfloat16).reshape(rows, steps, -1)


def power_of_two(number):
    return number > 0 and number & (number - 1) == 0


def fits(
    devices, normed_input, query_weight, query_gain, image_cache, tile_count, image_first_slot,
    cross_tile_mask, output_weight, output_gate,
):
    rows, steps, _ = normed_input.shape
    head_size = query_gain.shape[0]
    heads = query_weight.shape[1] // head_size
    kv_heads = image_cache.shape[2] // 2 // head_size
    if devices % 2 or heads % devices or image_cache.shape[0] != 1:
        return False
    tile = heads // devices * steps
    return (
        tile % 8 == 0
        and head_size % 128 == 0
        and rows * steps % 16 == 0
        and devices % kv_heads == 0
        and all(power_of_two(n) for n in (rows, steps, tile, devices))
        and query_weight.size + image_cache.size + output_weight.size <= 14 * 2**20
    )


def chosen(devices, *arrays):
    if fits(devices, *arrays):
        return fused_body(devices, *arrays)
    return body(*arrays)


def solution(mesh):
    return jax.shard_map(
        functools.partial(chosen, mesh.shape["tensor"]),
        mesh=mesh,
        in_specs=(
            P("groups", None, "tensor"),
            P("tensor", None),
            P(),
            P(("groups", "tensor"), None, None),
            P("groups"),
            P("groups"),
            P("groups", None, None),
            P(None, "tensor"),
            P(),
        ),
        out_specs=P("groups", None, "tensor"),
        check_vma=False,
    )
```

```python
import functools
import math

import jax
import jax.numpy as jnp
from jax import lax
from jax.experimental import pallas as pl
from jax.experimental.pallas import tpu as pltpu
from jax.sharding import PartitionSpec as P

EPSILON = 1e-05
NEGATIVE_FLOOR = -1e30
MESH = pl.DeviceIdType.MESH


def membership(image_first_slot, tile_count, pool_slots):
    ends = image_first_slot + tile_count
    return (pool_slots[:, None] >= image_first_slot[None, :]) & (
        pool_slots[:, None] < ends[None, :]
    )


def active_status(member_flag, image_first_slot, cross_tile_mask, pool_slots):
    member_int = member_flag.astype(jnp.int32)
    tile_index = jnp.sum(member_int * (pool_slots[:, None] - image_first_slot[None, :]), axis=1)
    row_masks = jnp.sum(member_int[:, :, None, None] * cross_tile_mask[None], axis=1)
    positions = jnp.arange(cross_tile_mask.shape[2], dtype=jnp.int32)
    chosen = jnp.sum(
        jnp.where(positions[None, None, :] == tile_index[:, None, None], row_masks, 0), axis=2
    )
    return (tile_index[:, None] == 0) | (chosen == 1)


def tile_partial(query_rows, cache_tile, head_size):
    steps = query_rows.shape[0]
    kv_width = cache_tile.shape[1] // 2
    kv_heads = kv_width // head_size
    group = query_rows.shape[1] // kv_width
    grouped = query_rows.reshape(steps, kv_heads, group, head_size)
    keys = cache_tile[:, :kv_width].reshape(-1, kv_heads, head_size)
    values = cache_tile[:, kv_width:].reshape(-1, kv_heads, head_size)
    scores = jnp.einsum("skgd,tkd->skgt", grouped, keys, preferred_element_type=jnp.float32) * (
        1.0 / math.sqrt(head_size)
    )
    tops = jnp.max(scores, axis=3)
    weights = jnp.exp(scores - tops[..., None]).astype(jnp.bfloat16)
    totals = jnp.sum(weights.astype(jnp.float32), axis=3)
    mixed = jnp.einsum("skgt,tkd->skgd", weights, values, preferred_element_type=jnp.float32)
    return (tops.reshape(steps, -1), totals.reshape(steps, -1), mixed.reshape(steps, -1))


def finish(numer_pairs, denom_pairs, head_size):
    pairs = numer_pairs.shape[0]
    heads = denom_pairs.shape[1]
    shaped = numer_pairs.reshape(pairs, heads, head_size) / denom_pairs[..., None]
    return shaped.astype(jnp.bfloat16).reshape(pairs, heads * head_size)


def body(
    normed_input,
    query_weight,
    query_gain,
    image_cache,
    tile_count,
    image_first_slot,
    cross_tile_mask,
    output_weight,
    output_gate,
):
    rows, steps, local_width = normed_input.shape
    head_size = query_gain.shape[0]
    heads = query_weight.shape[1] // head_size
    slot_count = image_cache.shape[0]
    flattened = normed_input.reshape(rows * steps, local_width)
    query = lax.psum_scatter(
        jnp.dot(flattened, query_weight, preferred_element_type=jnp.float32),
        "tensor",
        scatter_dimension=0,
        tiled=True,
    )
    shaped = query.reshape(slot_count, heads, head_size)
    normed = (
        shaped * lax.rsqrt(jnp.mean(shaped * shaped, axis=2, keepdims=True) + EPSILON) * query_gain
    )
    normed = normed.astype(jnp.bfloat16).reshape(slot_count, heads * head_size)
    all_queries = lax.all_gather(normed, "tensor", axis=0, tiled=True)
    target_device = lax.axis_index("tensor")
    pool_slots = target_device * slot_count + jnp.arange(slot_count, dtype=jnp.int32)
    member_flag = membership(image_first_slot, tile_count, pool_slots)
    active_entry = active_status(member_flag, image_first_slot, cross_tile_mask, pool_slots)
    by_row = all_queries.reshape(rows, steps * heads * head_size)
    selected = jnp.dot(member_flag.astype(jnp.bfloat16), by_row, preferred_element_type=jnp.float32)
    selected = selected.astype(jnp.bfloat16).reshape(slot_count, steps, heads * head_size)

    def slot_term(operands):
        return tile_partial(operands[0], operands[1], head_size)

    tops, totals, mixed = lax.map(slot_term, (selected, image_cache))
    masked = jnp.where(active_entry[:, :, None], tops, NEGATIVE_FLOOR)
    pair_index = target_device * slot_count + jnp.arange(slot_count, dtype=jnp.int32)
    pair_row = pair_index // steps
    pair_step = pair_index % steps
    gathered_tops, gathered_totals, gathered_mixed = (
        lax.all_gather(masked, "tensor", axis=0, tiled=True),
        lax.all_gather(totals, "tensor", axis=0, tiled=True),
        lax.all_gather(mixed, "tensor", axis=0, tiled=True),
    )
    all_slots = gathered_tops.shape[0]
    every_slot = jnp.arange(all_slots, dtype=jnp.int32)
    full_member = membership(image_first_slot, tile_count, every_slot)
    slot_pick = full_member[:, pair_row]
    step_pick = jnp.arange(steps, dtype=jnp.int32)[None, :] == pair_step[:, None]
    chosen = slot_pick[:, :, None] & step_pick[None, :, :]
    spread = jnp.where(chosen[..., None], gathered_tops[:, None, :, :], NEGATIVE_FLOOR)
    pair_max = jnp.max(spread, axis=(0, 2))
    weights = jnp.where(chosen[..., None], jnp.exp(spread - pair_max[None, :, None, :]), 0.0)
    denom_pairs = jnp.sum(weights * gathered_totals[:, None, :, :], axis=(0, 2))
    mixed_heads = gathered_mixed.reshape(all_slots, steps, heads, head_size)
    numer_pairs = jnp.einsum(
        "spth,sthd->phd", weights, mixed_heads, precision=lax.Precision.HIGHEST
    )
    numer_pairs = numer_pairs.reshape(slot_count, heads * head_size)
    attended = finish(numer_pairs, denom_pairs, head_size)
    projected = jnp.dot(
        lax.all_gather(attended, "tensor", axis=0, tiled=True),
        output_weight,
        preferred_element_type=jnp.float32,
    )
    result = jnp.tanh(output_gate[0]) * projected
    return result.astype(jnp.bfloat16).reshape(rows, steps, -1)


def fused_kernel(
    count_ref, first_ref, mask_ref, gate_ref, gain_ref, x_hbm, wq_hbm, cache_hbm, wo_hbm, out_ref,
    x_s, wq_s, kv_s, wo_s, send_a, recv_a, send_b, recv_b, send_c, recv_c, send_e, recv_e, live_s, att_s, att_all,
    x_sem, wq_sem, kv_sem, wo_sem, a_send, a_recv, b_send, b_recv, c_send, c_recv, e_send, e_recv,
    f_send, f_recv, p_send, p_recv,
    *, devices, kv_heads, steps, head_size,
):
    chips = devices // 2
    me = lax.axis_index("tensor")
    core = lax.rem(me, 2)
    chip = lax.div(me, 2)
    partner = me + 1 - 2 * core
    rows = x_s.shape[0]
    pairs = rows * steps
    width = wq_s.shape[2]
    local_heads = width // head_size
    tile = local_heads * steps
    block = rows * tile

    def remote(src, dst, send_sem, recv_sem, device):
        return pltpu.make_async_remote_copy(
            src_ref=src, dst_ref=dst, send_sem=send_sem, recv_sem=recv_sem,
            device_id={"tensor": device}, device_id_type=MESH,
        )

    def at(index, size):
        return pl.ds(pl.multiple_of(index * size, size), size)

    def flip(index, bits, count):
        total = 0
        for k in range(count.bit_length() - 1):
            bit = lax.rem(lax.div(index, 2**k), 2)
            total = total + (1 - bit if bits >> k & 1 else bit) * 2**k
        return total

    ahead = [flip(chip, chips - 1 - i, chips) for i in range(chips)]
    x_copy = pltpu.make_async_copy(x_hbm, x_s, x_sem.at[0])
    x_copy.start()
    lag = 2
    order = []
    for i in range(chips + lag):
        if i < chips:
            order.append((i, 0))
        if i >= lag:
            order.append((i - lag, 1))
    wq_copies = {}
    for i, own in order:
        b = 2 * ahead[i] + (core if own else 1 - core)
        n = 2 * i + own
        wq_copies[n] = pltpu.make_async_copy(
            wq_hbm.at[:, at(b, width)], wq_s.at[n], wq_sem.at[n]
        )
        wq_copies[n].start()

    barrier = pltpu.get_barrier_semaphore()
    for j in range(1, devices):
        pl.semaphore_signal(
            barrier, inc=1, device_id={"tensor": flip(me, j, devices)}, device_id_type=MESH
        )
    x_copy.wait()
    x = x_s[...].astype(jnp.float32).reshape(pairs, x_s.shape[2]).astype(jnp.bfloat16)
    a_copies = [
        remote(send_a.at[i], recv_a.at[i], a_send.at[i], a_recv.at[i], partner) for i in range(chips)
    ]
    b_copies = [
        remote(send_b.at[i], recv_b.at[i], b_send.at[i], b_recv.at[i], 2 * ahead[i] + core)
        for i in range(chips - 1)
    ]
    query = None
    for i, own in order:
        wq_copies[2 * i + own].wait()
        part = jnp.dot(x, wq_s[2 * i + own], preferred_element_type=jnp.float32)
        if not own:
            send_a[i] = part
            if i == 0:
                pl.semaphore_wait(barrier, devices - 1)
            a_copies[i].start()
            continue
        a_copies[i].wait_recv()
        part = part + recv_a[i]
        if i < chips - 1:
            send_b[i] = part
            b_copies[i].start()
        else:
            query = part

    kv_copy = pltpu.make_async_copy(cache_hbm.at[0], kv_s, kv_sem.at[0])
    kv_copy.start()
    wo_copy = pltpu.make_async_copy(wo_hbm, wo_s, wo_sem.at[0])
    wo_copy.start()

    shape = (devices * tile, local_heads * pairs)
    row_at = lax.broadcasted_iota(jnp.int32, shape, 0)
    column_at = lax.broadcasted_iota(jnp.int32, shape, 1)
    slot_at = row_at >> (tile.bit_length() - 1)
    inner = row_at & (tile - 1)
    pair_at = column_at & (pairs - 1)
    row_of = jnp.zeros(shape, jnp.int32)
    for r in range(rows):
        low = first_ref[r]
        row_of = jnp.where((slot_at >= low) & (slot_at < low + count_ref[r]), r, row_of)
    wanted = (row_of * steps + (inner & (steps - 1)) == pair_at) & (
        inner >> (steps.bit_length() - 1) == column_at >> (pairs.bit_length() - 1)
    )
    pick = jnp.where(wanted, 1.0, 0.0).astype(jnp.bfloat16)

    whole = (devices, tile, head_size)
    slot_at = lax.broadcasted_iota(jnp.int32, whole, 0)
    step_at = lax.broadcasted_iota(jnp.int32, whole, 1) & (steps - 1)
    live_row = jnp.full(whole, -1, jnp.int32)
    for r in range(rows):
        tile_at = slot_at - first_ref[r]
        allowed = jnp.where(tile_at == 0, 1, 0)
        for t in range(1, mask_ref.shape[1]):
            for s in range(steps):
                allowed = jnp.where((tile_at == t) & (step_at == s), mask_ref[s, t, r], allowed)
        live_row = jnp.where((tile_at < count_ref[r]) & (allowed == 1), r, live_row)
    live_s[...] = live_row

    for i in range(chips - 1):
        b_copies[i].wait_recv()
        query = query + recv_b[i]
    gain = gain_ref[...]
    normed = []
    for h in range(local_heads):
        part = query[:, h * head_size : (h + 1) * head_size]
        mean = jnp.mean(part * part, axis=1, keepdims=True)
        normed.append((part * lax.rsqrt(mean + EPSILON) * gain).astype(jnp.bfloat16))
    send_c[...] = jnp.dot(
        pick, jnp.concatenate(normed, axis=0), preferred_element_type=jnp.float32
    )
    c_copies = []
    for j in reversed(range(1, devices)):
        device = flip(me, j, devices)
        c_copies.append(
            remote(
                send_c.at[at(device, tile)], recv_c.at[at(me, tile)],
                c_send.at[j], c_recv.at[j], device,
            )
        )
        c_copies[-1].start()
    recv_c[at(me, tile), :] = send_c[at(me, tile), :]
    kv_copy.wait()
    for copy in c_copies:
        copy.wait_recv()

    group_rows = devices * tile // kv_heads
    kv_width = kv_heads * head_size
    lane = lax.broadcasted_iota(jnp.int32, (group_rows, head_size), 1)
    e_copies = []
    for i in range(chips):
        g = ahead[i]
        keys = kv_s[:, at(g, head_size)]
        values = kv_s[:, at(g + kv_heads, head_size)]
        scores = lax.dot_general(
            recv_c[at(g, group_rows), :].astype(jnp.bfloat16), keys, (((1,), (1,)), ((), ())),
            preferred_element_type=jnp.float32,
        ) * (1.0 / math.sqrt(head_size))
        top = jnp.max(scores, axis=1, keepdims=True)
        weights = jnp.exp(scores - top).astype(jnp.bfloat16)
        sums = jnp.sum(weights.astype(jnp.float32), axis=1, keepdims=True)
        mixed = jnp.dot(weights, values, preferred_element_type=jnp.float32)
        stats = jnp.where(lane < head_size // 2, top, sums)
        for n in range(2):
            send_e[i, n, :tile, :] = mixed[n * tile : (n + 1) * tile]
            send_e[i, n, tile:, :] = stats[n * tile : (n + 1) * tile]
        for other in range(2):
            side = 1 - core if other else core
            if i == chips - 1 and not other:
                recv_e[me] = send_e[i, core]
                continue
            e_copies.append(
                remote(
                    send_e.at[i, side], recv_e.at[me],
                    e_send.at[2 * i + other], e_recv.at[2 * i + other], 2 * g + side,
                )
            )
            e_copies[-1].start()
    for copy in e_copies:
        copy.wait_recv()

    mixes = recv_e[:, :tile, :]
    stats = recv_e[:, tile:, :]
    whole = (devices, tile, head_size)
    tops = jnp.broadcast_to(stats[:, :, 0:1], whole)
    sums = jnp.broadcast_to(stats[:, :, head_size // 2 : head_size // 2 + 1], whole)
    live_row = live_s[...]
    peaks = jnp.zeros(whole, jnp.float32)
    for r in range(rows):
        here = live_row == r
        peak = jnp.max(jnp.where(here, tops, NEGATIVE_FLOOR), axis=0, keepdims=True)
        peaks = jnp.where(here, peak, peaks)
    alive = live_row >= 0
    factor = jnp.where(alive, jnp.exp(jnp.where(alive, tops - peaks, 0.0)), 0.0)
    mixes = factor * mixes
    sums = factor * sums
    for r in range(rows):
        here = live_row == r
        numer = jnp.sum(jnp.where(here, mixes, 0.0), axis=0)
        denom = jnp.sum(jnp.where(here, sums, 0.0), axis=0)
        att_s[r * tile : (r + 1) * tile, :] = numer / denom

    to = lax.broadcasted_iota(jnp.int32, (block, block), 0)
    fro = lax.broadcasted_iota(jnp.int32, (block, block), 1)
    to_head = to >> (pairs.bit_length() - 1)
    to_pair = to & (pairs - 1)
    source = (
        (to_pair >> (steps.bit_length() - 1)) * tile + to_head * steps + (to_pair & (steps - 1))
    )
    swap = jnp.where(source == fro, 1.0, 0.0).astype(jnp.bfloat16)
    att_all[at(me, block), :] = jnp.dot(
        swap, att_s[...].astype(jnp.bfloat16), preferred_element_type=jnp.float32
    ).astype(jnp.bfloat16)

    f_copies = [
        remote(
            att_all.at[at(me, block)], att_all.at[at(me, block)],
            f_send.at[i], f_recv.at[i], 2 * ahead[i] + core,
        )
        for i in range(chips - 1)
    ]
    arrived = [me] + [2 * ahead[i] + core for i in range(chips - 1)]
    p_copies = [
        remote(
            att_all.at[at(b, block)], att_all.at[at(b, block)], p_send.at[n], p_recv.at[n], partner
        )
        for n, b in enumerate(arrived)
    ]
    p_copies[0].start()
    for copy in f_copies:
        copy.start()
    wo_copy.wait()

    def projected(b):
        heads = att_all[at(b, block), :]
        joined = jnp.concatenate(
            [heads[h * pairs : (h + 1) * pairs] for h in range(local_heads)], axis=1
        )
        return jnp.dot(joined, wo_s[at(b, width), :], preferred_element_type=jnp.float32)

    result = projected(me)
    for i in range(chips - 1):
        f_copies[i].wait_recv()
        p_copies[i + 1].start()
        result = result + projected(arrived[i + 1])
    for n in range(chips):
        p_copies[n].wait_recv()
        result = result + projected(arrived[n] + 1 - 2 * core)
    gate = jnp.tanh(jnp.full((1, width), gate_ref[0], jnp.float32))
    out_ref[...] = (gate * result).reshape(out_ref.shape).astype(out_ref.dtype)
    for copy in a_copies + b_copies + c_copies + e_copies + f_copies + p_copies:
        copy.wait_send()


def fused_body(
    devices,
    normed_input,
    query_weight,
    query_gain,
    image_cache,
    tile_count,
    image_first_slot,
    cross_tile_mask,
    output_weight,
    output_gate,
):
    rows, steps, local_width = normed_input.shape
    head_size = query_gain.shape[0]
    tokens, cache_width = image_cache.shape[1:]
    width = query_weight.shape[1] // devices
    pairs = rows * steps
    tile = width // head_size * steps
    chips = devices // 2
    dma = pltpu.SemaphoreType.DMA
    smem = pl.BlockSpec(memory_space=pltpu.SMEM)
    vmem = pl.BlockSpec(memory_space=pltpu.VMEM)
    hbm = pl.BlockSpec(memory_space=pl.ANY)
    return pl.pallas_call(
        functools.partial(
            fused_kernel, devices=devices, kv_heads=cache_width // 2 // head_size, steps=steps,
            head_size=head_size,
        ),
        out_shape=jax.ShapeDtypeStruct((rows, steps, output_weight.shape[1]), jnp.bfloat16),
        in_specs=[smem, smem, smem, smem, vmem, hbm, hbm, hbm, hbm],
        out_specs=vmem,
        scratch_shapes=[
            pltpu.VMEM((rows, steps, local_width), jnp.bfloat16),
            pltpu.VMEM((devices, local_width, width), jnp.bfloat16),
            pltpu.VMEM((tokens, cache_width), jnp.bfloat16),
            pltpu.VMEM(output_weight.shape, jnp.bfloat16),
            pltpu.VMEM((chips, pairs, width), jnp.float32),
            pltpu.VMEM((chips, pairs, width), jnp.float32),
            pltpu.VMEM((chips - 1, pairs, width), jnp.float32),
            pltpu.VMEM((chips - 1, pairs, width), jnp.float32),
            pltpu.VMEM((devices * tile, head_size), jnp.float32),
            pltpu.VMEM((devices * tile, head_size), jnp.float32),
            pltpu.VMEM((chips, 2, 2 * tile, head_size), jnp.float32),
            pltpu.VMEM((devices, 2 * tile, head_size), jnp.float32),
            pltpu.VMEM((devices, tile, head_size), jnp.int32),
            pltpu.VMEM((rows * tile, head_size), jnp.float32),
            pltpu.VMEM((devices * rows * tile, head_size), jnp.bfloat16),
            dma((1,)), dma((devices,)), dma((1,)), dma((1,)),
            dma((chips,)), dma((chips,)), dma((chips,)), dma((chips,)),
            dma((devices,)), dma((devices,)), dma((devices,)), dma((devices,)),
            dma((chips,)), dma((chips,)), dma((chips,)), dma((chips,)),
        ],
        compiler_params=pltpu.CompilerParams(collective_id=0, has_side_effects=True),
        name="gated_cross_attention",
    )(
        tile_count, image_first_slot, cross_tile_mask.transpose(1, 2, 0), output_gate,
        query_gain.reshape(1, head_size), normed_input, query_weight, image_cache, output_weight,
    )


def power_of_two(number):
    return number > 0 and number & (number - 1) == 0


def fits(
    devices, normed_input, query_weight, query_gain, image_cache, tile_count, image_first_slot,
    cross_tile_mask, output_weight, output_gate,
):
    rows, steps, _ = normed_input.shape
    head_size = query_gain.shape[0]
    heads = query_weight.shape[1] // head_size
    kv_heads = image_cache.shape[2] // 2 // head_size
    if devices % 2 or heads % devices or image_cache.shape[0] != 1:
        return False
    tile = heads // devices * steps
    return (
        tile % 8 == 0
        and head_size % 128 == 0
        and rows * steps % 16 == 0
        and devices == 2 * kv_heads
        and all(power_of_two(n) for n in (rows, steps, tile, devices))
        and query_weight.size + image_cache.size + output_weight.size <= 14 * 2**20
    )


def chosen(devices, *arrays):
    if fits(devices, *arrays):
        return fused_body(devices, *arrays)
    return body(*arrays)


def solution(mesh):
    return jax.shard_map(
        functools.partial(chosen, mesh.shape["tensor"]),
        mesh=mesh,
        in_specs=(
            P("groups", None, "tensor"),
            P("tensor", None),
            P(),
            P(("groups", "tensor"), None, None),
            P("groups"),
            P("groups"),
            P("groups", None, None),
            P(None, "tensor"),
            P(),
        ),
        out_specs=P("groups", None, "tensor"),
        check_vma=False,
    )
```
